128 devices in a mesh: space: 64 (over z, y, x_lo, core), mem: 2 (over x_hi).
Axes of the slice: x: 4 (x_hi: 2, x_lo: 2; x = x_hi * 2 + x_lo), y: 4, z: 4, core: 2. Of those that a mesh axis runs over, the one named last changes fastest.
Arguments:
- state: float32 [64, 1048576], P('mem', 'space'), may hold values from -6 to 6
- obs_index: int32 [4, 16384], P(None, 'space'), may hold values from 0 to 1048575, as said below
- obs_value: float32 [4, 16384], P(None, 'space'), may hold values from -8 to 8
- obs_var: float32 [4, 16384], P(None, 'space'), may hold values from 0.02 to 5
Outputs:
- posterior: float32 [64, 1048576], P('mem', 'space')
The draws below stay inside these ranges and needn't reach their ends.
Inputs may be any that keep to these rules, and one draw needn't show every extreme that they name: `obs_index`: observation k of every batch measures a column of the block owned by index k // 256 of space, that is a column between (k // 256) * 16384 and (k // 256 + 1) * 16384 - 1.
All inputs are finite; a program needn't handle non-finite values.
Results may differ from the reference program's by a relative error of at most 0.0075.
Values may be sent and summed in bfloat16 or wider, within the bound.
No kernel may reach another device: no remote copies, remote signals or barrier semaphores. Data moves between devices by JAX's collectives and lax.ppermute only.
A program may use at most 64 MiB of HBM per device.

```python
import math
import jax
import jax.numpy as jnp
from jax import lax

M = 64
COLS = 16384
OBS_DEV = 256
BATCHES = 4
STATE = 1048576
OBS = 16384
RADIUS = 32768
N_SPACE = 64


def draw_obs_index(key, part):
    blocks = OBS // OBS_DEV
    key_kind, key_place, key_offset = jax.random.split(key, 3)
    scattered = jax.random.randint(key_kind, (BATCHES, blocks), 0, 4, dtype=jnp.int32) == 0
    window = jnp.where(scattered, COLS, 2 * OBS_DEV).astype(jnp.int32)
    window_start = jax.random.randint(key_place, (BATCHES, blocks), 0, 1 << 30, dtype=jnp.int32) % (COLS - window + 1)
    window_full = jnp.repeat(window, OBS_DEV, axis=1)
    start_full = jnp.repeat(window_start, OBS_DEV, axis=1)
    raw_offset = jax.random.randint(key_offset, (BATCHES, OBS), 0, 1 << 30, dtype=jnp.int32)
    offsets = start_full + raw_offset % window_full
    owners = jnp.arange(OBS, dtype=jnp.int32) // OBS_DEV
    slot_index = jnp.arange(OBS, dtype=jnp.int32)[None, :]
    offsets = jnp.where(slot_index == 0, 0, offsets)
    offsets = jnp.where(slot_index == OBS - 1, COLS - 1, offsets)
    return (owners[None, :] * COLS + offsets).astype(jnp.int32)


def draw_obs_var(key, part):
    key_phase, key_level = jax.random.split(key)
    owners = jnp.arange(OBS, dtype=jnp.int32) // OBS_DEV
    phase = jax.random.randint(key_phase, (BATCHES, 1), 0, 4, dtype=jnp.int32)
    precise = (owners[None, :] + phase) % 4 == 0
    fraction = jax.random.uniform(key_level, (BATCHES, OBS), jnp.float32)
    sharp = 0.02 * jnp.exp(fraction * math.log(5.0))
    loose = jnp.exp(fraction * math.log(5.0))
    return jnp.where(precise, sharp, loose).astype(jnp.float32)


def level_of(stream_key, dims, pieces, low, high):
    level = 1.0
    for position, shards_of in pieces:
        heights = jax.random.uniform(jax.random.fold_in(jax.random.fold_in(stream_key, 6), position), (shards_of,), jnp.float32, low / len(pieces), high / len(pieces))
        level = level * jnp.repeat(jnp.exp(heights), dims[position] // shards_of).reshape((-1,) + (1,) * (len(dims) - 1 - position))
    return level


def scatter_about(stream_key, extent, scale, most, cuts=(), held_as=jnp.bfloat16):
    drawn = jax.random.normal(stream_key, extent, jnp.float32) * scale
    if len(cuts) > 0:
        drawn = level_of(stream_key, extent, cuts, -0.22, 0.18) * drawn
    return jnp.clip(drawn, min=-most, max=most).astype(held_as)


def setup_inputs(seed: int = 0) -> dict:
    streams_of = jax.random.split(jax.random.key(seed), 5)
    state = scatter_about(streams_of[0], (M, STATE), 1.0, 6.0, ((0, 2), (1, 64)), jnp.float32)
    obs_index = draw_obs_index(jax.random.fold_in(streams_of[4], 71), 0)
    obs_value = scatter_about(streams_of[2], (BATCHES, OBS), 1.5, 8.0, ((1, 64),), jnp.float32)
    obs_var = draw_obs_var(jax.random.fold_in(streams_of[4], 71), 0)
    return {"state": state, "obs_index": obs_index, "obs_value": obs_value, "obs_var": obs_var}


def summarize(prior_obs, values, variances):
    members = prior_obs.shape[0]
    obs_mean = lax.optimization_barrier(jnp.mean(prior_obs, axis=0))
    anomaly = prior_obs - obs_mean
    spread = lax.optimization_barrier(jnp.sum(anomaly * anomaly, axis=0)) / (members - 1) + 1e-06
    post_var = 1.0 / (1.0 / spread + 1.0 / variances)
    post_mean = post_var * (obs_mean / spread + values / variances)
    change = post_mean - obs_mean + (jnp.sqrt(post_var / spread) - 1.0) * anomaly
    weighted = (change / ((members - 1) * spread)).astype(jnp.bfloat16)
    return (anomaly.astype(jnp.bfloat16), weighted)

def reference(state, obs_index, obs_value, obs_var):
    members = state.shape[0]
    current = state
    margin = 2 * OBS_DEV
    for batch in range(BATCHES):
        positions = obs_index[batch]
        prior_obs = current[:, positions]
        anomaly, weighted = summarize(prior_obs, obs_value[batch], obs_var[batch])
        anomaly_pad = jnp.pad(anomaly, ((0, 0), (margin, margin)))
        weighted_pad = jnp.pad(weighted, ((0, 0), (margin, margin)))
        position_pad = jnp.pad(positions, (margin, margin))
        state_anom = (current - lax.optimization_barrier(jnp.mean(current, axis=0))).astype(jnp.bfloat16)
        spread_blocks = jnp.transpose(state_anom.reshape(members, N_SPACE, COLS), (1, 0, 2))

        def one_block(inputs):
            column_block, spread_piece = inputs
            band_start = (column_block * OBS_DEV).astype(jnp.int32)
            band_anom = lax.dynamic_slice_in_dim(anomaly_pad, band_start, 5 * OBS_DEV, 1)
            band_weight = lax.dynamic_slice_in_dim(weighted_pad, band_start, 5 * OBS_DEV, 1)
            band_pos = lax.dynamic_slice_in_dim(position_pad, band_start, 5 * OBS_DEV, 0)
            cov = jnp.dot(band_anom.T, spread_piece, preferred_element_type=jnp.float32)
            column_pos = (column_block * COLS).astype(jnp.int32) + lax.iota(jnp.int32, COLS)
            distance = jnp.abs(column_pos[None, :] - band_pos[:, None]).astype(jnp.float32)
            taper = jnp.square(jnp.maximum(0.0, 1.0 - distance / RADIUS))
            gain = (taper * cov).astype(jnp.bfloat16)
            return jnp.dot(band_weight, gain, preferred_element_type=jnp.float32)
        deltas = lax.map(one_block, (jnp.arange(N_SPACE, dtype=jnp.int32), spread_blocks))
        current = current + jnp.transpose(deltas, (1, 0, 2)).reshape(members, N_SPACE * COLS)
    return current
```

```python
import functools

import jax
import jax.numpy as jnp
from jax import lax
from jax.experimental import pallas as pl
from jax.experimental.pallas import tpu as pltpu
from jax.sharding import PartitionSpec as P

RADIUS = 32768
OFFSETS = (-2, -1, 0, 1, 2)
CHUNK = 1024
WINDOW = 64
LANES = 128
FAR_AWAY = 100.0
BF16 = jnp.bfloat16
F32 = jnp.float32


def vmem_call(body, outs, ins, scratch=(), aliases=None, name=None, cost=None):
    return pl.pallas_call(
        body,
        out_shape=outs,
        in_specs=ins,
        out_specs=jax.tree.map(lambda _: pl.BlockSpec(memory_space=pltpu.VMEM), outs),
        scratch_shapes=list(scratch),
        input_output_aliases=aliases or {},
        compiler_params=pltpu.CompilerParams(vmem_limit_bytes=48 << 20),
        cost_estimate=cost,
        name=name,
    )


VM = pl.BlockSpec(memory_space=pltpu.VMEM)
SM = pl.BlockSpec(memory_space=pltpu.SMEM)


def cost(flops, moved):
    return pl.CostEstimate(flops=int(flops), bytes_accessed=int(moved), transcendentals=0)


def prep_body(half_ref, table_ref, x_ref, tracked_ref, sorted_ref, keep_ref, send_ref, mean_ref):
    batches = table_ref.shape[0] // 4
    count = table_ref.shape[1]
    rows = table_ref[...]
    cols = jnp.transpose(rows)
    sub = lax.broadcasted_iota(jnp.int32, (count, count), 0).astype(F32)
    lane = lax.broadcasted_iota(jnp.int32, (count, count), 1).astype(F32)
    del sub
    for b in range(batches):
        key_row = rows[b : b + 1]
        key_col = cols[:, b : b + 1]
        rank_col = jnp.sum(jnp.where(key_row < key_col, 1.0, 0.0), axis=1, keepdims=True)
        hit = rank_col == lane
        for q in range(3):
            piece = cols[:, (q + 1) * batches + b : (q + 1) * batches + b + 1]
            sorted_ref[q * batches + b : q * batches + b + 1, :] = jnp.sum(
                jnp.where(hit, piece, 0.0), axis=0, keepdims=True
            )
    tiles = batches * count // LANES
    members = x_ref.shape[0]
    index = []
    for t in range(tiles):
        b, start = divmod(t * LANES, count)
        pos = sorted_ref[b : b + 1, start : start + LANES].astype(jnp.int32)
        index.append(jnp.broadcast_to(pos, (8, LANES)))
    high = [i // LANES for i in index]
    low = [i % LANES for i in index]

    for group in range(members // 8):
        lines = slice(group * 8, group * 8 + 8)

        def visit(q, found, lines=lines):
            piece = x_ref[lines, pl.ds(pl.multiple_of(q * LANES, LANES), LANES)]
            new = []
            for t in range(tiles):
                picked = jnp.take_along_axis(piece, low[t], axis=1)
                new.append(jnp.where(high[t] == q, picked, found[t]))
            return tuple(new)

        zero = jnp.zeros((8, LANES), F32)
        found = lax.fori_loop(0, x_ref.shape[1] // LANES, visit, (zero,) * tiles, unroll=4)
        for t in range(tiles):
            tracked_ref[lines, t * LANES : (t + 1) * LANES] = found[t]

    half = half_ref[0]
    width = keep_ref.shape[1]
    step = 2048

    def split(i, carry):
        at = pl.ds(pl.multiple_of(i * step, step), step)
        here = pl.ds(pl.multiple_of(half * width + i * step, step), step)
        there = pl.ds(pl.multiple_of((1 - half) * width + i * step, step), step)
        keep_ref[:, at] = x_ref[:, here]
        out = x_ref[:, there]
        mean = jnp.sum(out, axis=0, keepdims=True) * (1.0 / members)
        mean_ref[:, at] = mean
        send_ref[:, at] = (out - mean).astype(BF16)
        return carry

    lax.fori_loop(0, width // step, split, 0)


def summary_rows(prior, values, variances):
    members = prior.shape[0]
    obs_mean = jnp.sum(prior, axis=0, keepdims=True) / members
    anomaly = prior - obs_mean
    spread = jnp.sum(anomaly * anomaly, axis=0, keepdims=True) / (members - 1) + 1e-06
    post_var = 1.0 / (1.0 / spread + 1.0 / variances)
    post_mean = post_var * (obs_mean / spread + values / variances)
    change = post_mean - obs_mean + (jnp.sqrt(post_var / spread) - 1.0) * anomaly
    weighted = change / ((members - 1) * spread)
    return jnp.concatenate([anomaly, weighted], axis=0)


def first_body(own_ref, other_ref, sorted_ref, tracked_ref, pay_ref):
    tracked_ref[: own_ref.shape[0], :] = own_ref[...]
    tracked_ref[own_ref.shape[0] :, :] = other_ref[...]
    count = sorted_ref.shape[1]
    batches = sorted_ref.shape[0] // 3
    prior = tracked_ref[:, :count]
    both = summary_rows(
        prior, sorted_ref[batches : batches + 1, :], sorted_ref[2 * batches : 2 * batches + 1, :]
    )
    pay_ref[:count, :] = jnp.transpose(both).astype(BF16)
    pos = sorted_ref[:batches, :].astype(jnp.int32)
    pieces = [pos[:, i * LANES : (i + 1) * LANES] for i in range(count // LANES)]
    pos = jnp.concatenate(pieces, axis=0)
    pay_ref[count:, :] = jnp.concatenate(
        [(pos // LANES).astype(F32), (pos % LANES).astype(F32)], axis=0
    ).astype(BF16)


def taper_of(position, column):
    near = jnp.maximum(1.0 - jnp.abs(column - position), 0.0)
    return near * near


def step_body(batch, aw0, aw1, aw2, aw3, aw4, pcol_ref, sorted_ref, old_ref, new_ref, pay_ref):
    count = sorted_ref.shape[1]
    batches = sorted_ref.shape[0] // 3
    old = old_ref[:, count:]
    members = old.shape[0]
    mean = jnp.sum(old, axis=0, keepdims=True) * (1.0 / members)
    anom = (old - mean).astype(BF16)
    column = jnp.concatenate([sorted_ref[b : b + 1, :] for b in range(batch, batches)], axis=1)
    column = column * (1.0 / RADIUS)
    total = old
    for o, aw_ref in enumerate((aw0, aw1, aw2, aw3, aw4)):
        at = aw_ref[:count, :members]
        wt = aw_ref[:count, members:]
        cov = jnp.dot(at, anom, preferred_element_type=F32)
        position = pcol_ref[o * count : (o + 1) * count, batch - 1 : batch]
        gain = (taper_of(position, column) * cov).astype(BF16)
        total = total + lax.dot_general(
            wt, gain, (((0,), (0,)), ((), ())), preferred_element_type=F32
        )
    new_ref[...] = total
    both = summary_rows(
        total[:, :count],
        sorted_ref[batches + batch : batches + batch + 1, :],
        sorted_ref[2 * batches + batch : 2 * batches + batch + 1, :],
    )
    pay_ref[...] = jnp.transpose(both).astype(BF16)


def bulk_body(
    batch, first, table_ref, aw0, aw1, aw2, aw3, aw4, pcol_ref, prow_ref, *rest
):
    if first:
        keep_ref, dev_ref, mean_ref, x_ref, w_ref, at_ref, gain_ref = rest
    else:
        old_ref, x_ref, w_ref, at_ref, gain_ref = rest
    aws = (aw0, aw1, aw2, aw3, aw4)
    count = pcol_ref.shape[0] // len(OFFSETS)
    members = x_ref.shape[0]
    total = count * len(OFFSETS)
    for o, aw_ref in enumerate(aws):
        both = jnp.transpose(aw_ref[:count, :].astype(F32))
        w_ref[:, o * count : (o + 1) * count] = both[members:, :]
        at_ref[o * count : (o + 1) * count, :] = aw_ref[:count, :members]
    position_row = prow_ref[batch : batch + 1, :]
    place = lax.broadcasted_iota(jnp.int32, (1, total), 1)
    ramp = (
        lax.broadcasted_iota(jnp.int32, (1, CHUNK), 1).astype(F32) - (CHUNK // 2)
    ) * (1.0 / RADIUS)
    half = table_ref[0]
    chunks = x_ref.shape[1] // CHUNK
    kinds = (0, 2, 4)
    base = half * x_ref.shape[1]

    def entry(c, kind, what):
        return table_ref[8 + ((batch * 3 + kind) * chunks + c) * 2 + what]

    def chunk(c, carry):
        span = pl.ds(pl.multiple_of(c * CHUNK, CHUNK), CHUNK)
        if first:
            x = jnp.concatenate(
                [keep_ref[:, span], dev_ref[:, span].astype(F32) + mean_ref[:, span]], axis=0
            )
        else:
            x = old_ref[:, span]
        mean = jnp.sum(x, axis=0, keepdims=True) * (1.0 / members)
        anom = (x - mean).astype(BF16)
        centre = (base + c * CHUNK + CHUNK // 2).astype(F32) * (1.0 / RADIUS)
        away = centre - position_row
        reach = 1.0 - jnp.abs(away)
        far = reach > 0.0
        starts = []
        for kind, o in enumerate(kinds):
            w0 = pl.multiple_of(entry(c, kind, 0), 16)
            starts.append(w0)
            lo = o * count + w0
            hi = lo + WINDOW * entry(c, kind, 1)
            far = far & ((place < lo) | (place >= hi))
        flat = jnp.where(far, 1.0, 0.0)
        reach = jnp.where(far, reach, 0.0)
        slope = jnp.where(away > 0.0, -2.0, 2.0) * reach
        weights = w_ref[...]
        scaled = jnp.concatenate(
            [
                (weights * (reach * reach)).astype(BF16),
                (weights * slope).astype(BF16),
                (weights * flat).astype(BF16),
            ],
            axis=0,
        )
        poly = jnp.dot(scaled, at_ref[...], preferred_element_type=F32).astype(BF16)
        near = [aws[o][pl.ds(starts[i], WINDOW), :] for i, o in enumerate(kinds)]
        lhs = jnp.concatenate([poly] + [n[:, :members] for n in near], axis=0)
        both = jnp.dot(lhs, anom, preferred_element_type=F32)
        column = centre + ramp
        for i, o in enumerate(kinds):
            position = pcol_ref[pl.ds(o * count + starts[i], WINDOW), batch : batch + 1]
            cov = both[3 * members + i * WINDOW : 3 * members + (i + 1) * WINDOW]
            gain_ref[i * WINDOW : (i + 1) * WINDOW, :] = (
                taper_of(position, column) * cov
            ).astype(BF16)
        wt = jnp.concatenate([n[:, members:] for n in near], axis=0)
        change = lax.dot_general(
            wt, gain_ref[...], (((0,), (0,)), ((), ())), preferred_element_type=F32
        )
        change = change + both[:members]
        change = change + ramp * (
            both[members : 2 * members] + ramp * both[2 * members : 3 * members]
        )
        x_ref[:, span] = x + change

        for i, o in enumerate(kinds):

            def more(n, carry, i=i, o=o):
                start = pl.multiple_of(starts[i] + n * WINDOW, 16)
                aw = aws[o][pl.ds(start, WINDOW), :]
                cov = jnp.dot(aw[:, :members], anom, preferred_element_type=F32)
                position = pcol_ref[pl.ds(o * count + start, WINDOW), batch : batch + 1]
                gain = (taper_of(position, column) * cov).astype(BF16)
                x_ref[:, span] = x_ref[:, span] + lax.dot_general(
                    aw[:, members:], gain, (((0,), (0,)), ((), ())), preferred_element_type=F32
                )
                return carry

            lax.fori_loop(1, entry(c, i, 1), more, 0)
        return carry

    lax.fori_loop(0, chunks, chunk, 0)


def cyclic(block, distance):
    n = lax.axis_size("space")
    return lax.ppermute(block, "space", [((i + distance) % n, i) for i in range(n)])


def band(block):
    return [block if o == 0 else cyclic(block, o) for o in OFFSETS]


def shards(state, obs_index, obs_value, obs_var):
    mem_index = lax.axis_index("mem")
    space_index = lax.axis_index("space")
    blocks = lax.axis_size("space")
    members_here, block_width = state.shape
    members = 2 * members_here
    width = block_width // 2
    batches, count = obs_index.shape
    swap = [(0, 1), (1, 0)]

    local = obs_index - space_index * block_width
    key = local * count + lax.broadcasted_iota(jnp.int32, local.shape, 1)
    table = jnp.concatenate([key.astype(F32), local.astype(F32), obs_value, obs_var], axis=0)
    half = mem_index.astype(jnp.int32).reshape(1)
    shape = jax.ShapeDtypeStruct
    own, srt, keep, send, mean = vmem_call(
        prep_body,
        (
            shape((members_here, batches * count), F32),
            shape((3 * batches, count), F32),
            shape((members_here, width), F32),
            shape((members_here, width), BF16),
            shape((1, width), F32),
        ),
        [SM, VM, VM],
        name="prep",
        cost=cost(1e7, 8e6),
    )(half, table, state)
    other = lax.ppermute(own, "mem", swap)
    dev = lax.ppermute(send, "mem", swap)
    dev_mean = lax.ppermute(mean, "mem", swap)

    tracked, pay = vmem_call(
        first_body,
        (shape((members, batches * count), F32), shape((count + 16, 2 * members), BF16)),
        [VM, VM, VM],
        name="first",
        cost=cost(1e6, 1e6),
    )(own, other, srt)

    aws = band(pay)
    position = jnp.stack([a[count:].astype(jnp.int32) for a in aws])
    position = position[:, :8] * LANES + position[:, 8:]
    position = position.reshape(5, count // LANES, batches, LANES).transpose(0, 2, 1, 3)
    position = position.reshape(5, batches, count)
    offset = jnp.asarray(OFFSETS, jnp.int32)
    source = space_index + offset
    valid = (source >= 0) & (source < blocks)
    relative = (position + (offset * block_width)[:, None, None]).astype(F32) * (1.0 / RADIUS)
    relative = jnp.where(valid[:, None, None], relative, FAR_AWAY)
    prow = relative.transpose(1, 0, 2).reshape(batches, 5 * count)
    pcol = prow.T

    chunks = width // CHUNK
    edges = mem_index * width + CHUNK * lax.iota(jnp.int32, chunks + 1)
    mixed = position[jnp.asarray((0, 2, 4))].transpose(1, 0, 2)
    below = jnp.sum((mixed[:, :, None, :] < edges[None, None, :, None]).astype(jnp.int32), axis=-1)
    k0, k1 = below[:, :, :-1], below[:, :, 1:]
    w0 = jnp.minimum(k0 // 16 * 16, count - WINDOW)
    nw = jnp.maximum((k1 - w0 + WINDOW - 1) // WINDOW, 1)
    w0 = jnp.minimum(w0, count - WINDOW * nw)
    windows = jnp.concatenate(
        [jnp.broadcast_to(half, (8,)), jnp.stack([w0, nw], axis=-1).reshape(-1)]
    )

    x = None
    for batch in range(batches):
        if batch + 1 < batches:
            later = (batches - batch - 1) * count
            tracked, pay = vmem_call(
                functools.partial(step_body, batch + 1),
                (shape((members, later), F32), shape((count, 2 * members), BF16)),
                [VM] * 8,
                name=f"step{batch + 1}",
                cost=cost(2 * 2 * 5 * count * members * later, 1e6),
            )(*aws, pcol, srt, tracked)
            following = band(pay)
        state_args = (keep, dev, dev_mean) if batch == 0 else (x,)
        x = vmem_call(
            functools.partial(bulk_body, batch, batch == 0),
            shape((members, width), F32),
            [SM] + [VM] * (7 + len(state_args)),
            scratch=[
                pltpu.VMEM((members, 5 * count), F32),
                pltpu.VMEM((5 * count, members), BF16),
                pltpu.VMEM((3 * WINDOW, CHUNK), BF16),
            ],
            name=f"bulk{batch}",
            cost=cost(2e9, 6e6),
        )(windows, *aws, pcol, prow, *state_args)
        if batch + 1 < batches:
            aws = following

    mine = x[:members_here]
    theirs = lax.ppermute(x[members_here:].astype(BF16), "mem", swap).astype(F32)
    first = mem_index == 0
    left = jnp.where(first, mine, theirs)
    right = jnp.where(first, theirs, mine)
    return jnp.concatenate([left, right], axis=1)


def solution(mesh):
    placed = (P("mem", "space"), P(None, "space"), P(None, "space"), P(None, "space"))
    return jax.shard_map(
        shards, mesh=mesh, in_specs=placed, out_specs=P("mem", "space"), check_vma=False
    )
```

```python
import functools

import jax
import jax.numpy as jnp
from jax import lax
from jax.experimental import pallas as pl
from jax.experimental.pallas import tpu as pltpu
from jax.sharding import PartitionSpec as P


RADIUS = 32768
OFFSETS = (-2, -1, 0, 1, 2)
CHUNK = 1024
WINDOW = 32
MORE = 128
PAD = 128
UNROLL = 2
PIECES = 2
KINDS = (0, 2, 4)
LANES = 128
FAR_AWAY = 100.0
BF16 = jnp.bfloat16
F32 = jnp.float32


def vmem_call(body, outs, ins, scratch=(), aliases=None, cost=None):
    return pl.pallas_call(
        body,
        out_shape=outs,
        in_specs=ins,
        out_specs=jax.tree.map(lambda _: pl.BlockSpec(memory_space=pltpu.VMEM), outs),
        scratch_shapes=list(scratch),
        input_output_aliases=aliases or {},
        compiler_params=pltpu.CompilerParams(vmem_limit_bytes=48 << 20),
        cost_estimate=cost,
    )


VM = pl.BlockSpec(memory_space=pltpu.VMEM)
SM = pl.BlockSpec(memory_space=pltpu.SMEM)


def cost(flops, moved):
    return pl.CostEstimate(flops=int(flops), bytes_accessed=int(moved), transcendentals=0)


def thirds(x):
    high = x.astype(BF16)
    rest = x - high.astype(F32)
    middle = rest.astype(BF16)
    return high, middle, (rest - middle.astype(F32)).astype(BF16)


def placement(rows, cols, b):
    count = rows.shape[1]
    rank = jnp.sum(
        jnp.where(cols[:, b : b + 1] < rows[b : b + 1], 1.0, 0.0), axis=0, keepdims=True
    )
    place = lax.broadcasted_iota(jnp.int32, (count, count), 0).astype(F32)
    return jnp.where(rank == place, 1.0, 0.0).astype(BF16)


def gather_batch(b, members, rows, cols, hot, index_ref, turned_ref, rows_ref):
    count = rows.shape[1]
    batches = rows.shape[0] // 4
    unroll = 16

    def pick(i, carry):
        for u in range(unroll):
            k = i * unroll + u
            rows_ref[pl.ds(k, 1), :] = turned_ref[pl.ds(index_ref[8 + b * count + k], 1), :]
        return carry

    lax.fori_loop(0, count // unroll, pick, 0)
    group = (cols[:, batches + b : batches + b + 1].astype(jnp.int32) // LANES) % (LANES // members)
    lane = lax.broadcasted_iota(jnp.int32, (count, LANES), 1) // members
    found = jnp.where(lane == group, rows_ref[...], 0.0)
    parts = [jnp.dot(hot, t, preferred_element_type=F32) for t in thirds(found)]
    placed = jnp.transpose((parts[0] + parts[1]) + parts[2])
    total = placed[:members]
    for g in range(1, LANES // members):
        total = total + placed[g * members : (g + 1) * members]
    return total


def prep_body(index_ref, table_ref, x_ref, turned_ref, own_ref, sorted_ref, rows_ref):
    batches = table_ref.shape[0] // 4
    members = x_ref.shape[0]
    groups = LANES // members

    def turn(i, carry):
        at = [
            pl.ds(pl.multiple_of((i * groups + g) * LANES, LANES), LANES) for g in range(groups)
        ]
        block = jnp.concatenate([x_ref[:, a] for a in at], axis=0)
        turned_ref[pl.ds(pl.multiple_of(i * LANES, LANES), LANES), :] = jnp.transpose(block)
        return carry

    lax.fori_loop(0, x_ref.shape[1] // (groups * LANES), turn, 0, unroll=2)
    rows = table_ref[...]
    cols = jnp.transpose(rows)
    for b in range(batches):
        hot = placement(rows, cols, b)
        values = jnp.concatenate([rows[(q + 1) * batches + b : (q + 1) * batches + b + 1] for q in range(3)], axis=0)
        parts = [
            lax.dot_general(t, hot, (((1,), (1,)), ((), ())), preferred_element_type=F32)
            for t in thirds(values)
        ]
        ordered = (parts[0] + parts[1]) + parts[2]
        for q in range(3):
            sorted_ref[q * batches + b : q * batches + b + 1, :] = ordered[q : q + 1]
        if b == 0:
            own_ref[...] = gather_batch(
                b, members, rows, cols, hot, index_ref, turned_ref, rows_ref
            )


def prep_rest_body(
    index_ref, table_ref, x_ref, turned_ref, own_ref, keep_ref, send_ref, mean_ref, rows_ref
):
    batches = table_ref.shape[0] // 4
    count = table_ref.shape[1]
    members = x_ref.shape[0]
    half = index_ref[0]
    width = keep_ref.shape[1]
    step = 2048

    def split(i, carry):
        at = pl.ds(pl.multiple_of(i * step, step), step)
        here = pl.ds(pl.multiple_of(half * width + i * step, step), step)
        there = pl.ds(pl.multiple_of((1 - half) * width + i * step, step), step)
        keep_ref[:, at] = x_ref[:, here]
        out = x_ref[:, there]
        mean = jnp.sum(out, axis=0, keepdims=True) * (1.0 / members)
        mean_ref[:, at] = mean
        send_ref[:, at] = (out - mean).astype(BF16)
        return carry

    lax.fori_loop(0, width // step, split, 0)
    rows = table_ref[...]
    cols = jnp.transpose(rows)
    for b in range(1, batches):
        hot = placement(rows, cols, b)
        own_ref[:, (b - 1) * count : b * count] = gather_batch(
            b, members, rows, cols, hot, index_ref, turned_ref, rows_ref
        )


def summary_rows(prior, values, variances):
    members = prior.shape[0]
    obs_mean = jnp.sum(prior, axis=0, keepdims=True) / members
    anomaly = prior - obs_mean
    spread = jnp.sum(anomaly * anomaly, axis=0, keepdims=True) / (members - 1) + 1e-06
    post_var = 1.0 / (1.0 / spread + 1.0 / variances)
    post_mean = post_var * (obs_mean / spread + values / variances)
    change = post_mean - obs_mean + (jnp.sqrt(post_var / spread) - 1.0) * anomaly
    weighted = change / ((members - 1) * spread)
    return jnp.concatenate([anomaly, weighted], axis=0)


def first_body(own_ref, other_ref, sorted_ref, pay_ref):
    count = sorted_ref.shape[1]
    batches = sorted_ref.shape[0] // 3
    prior = jnp.concatenate([own_ref[...], other_ref[...]], axis=0)
    both = summary_rows(
        prior, sorted_ref[batches : batches + 1, :], sorted_ref[2 * batches : 2 * batches + 1, :]
    )
    pay_ref[:count, :] = jnp.transpose(both).astype(BF16)
    pos = sorted_ref[:batches, :].astype(jnp.int32)
    pieces = [pos[:, i * LANES : (i + 1) * LANES] for i in range(count // LANES)]
    pos = jnp.concatenate(pieces, axis=0)
    pay_ref[count:, :] = jnp.concatenate(
        [(pos // LANES).astype(F32), (pos % LANES).astype(F32)], axis=0
    ).astype(BF16)


def taper_of(position, column):
    near = jnp.maximum(1.0 - jnp.abs(column - position), 0.0)
    return near * near


def step_body(batch, aw0, aw1, aw2, aw3, aw4, pcol_ref, sorted_ref, *rest):
    count = sorted_ref.shape[1]
    batches = sorted_ref.shape[0] // 3
    new_ref, pay_ref = rest[-2:]
    if batch == 1:
        old = jnp.concatenate([rest[0][...], rest[1][...]], axis=0)
    else:
        old = rest[0][:, count:]
    members = old.shape[0]
    mean = jnp.sum(old, axis=0, keepdims=True) * (1.0 / members)
    anom = (old - mean).astype(BF16)
    column = jnp.concatenate([sorted_ref[b : b + 1, :] for b in range(batch, batches)], axis=1)
    column = column * (1.0 / RADIUS)
    total = old
    for o, aw_ref in enumerate((aw0, aw1, aw2, aw3, aw4)):
        at = aw_ref[:count, :members]
        wt = aw_ref[:count, members:]
        cov = jnp.dot(at, anom, preferred_element_type=F32)
        position = pcol_ref[o * count : (o + 1) * count, batch - 1 : batch]
        gain = (taper_of(position, column) * cov).astype(BF16)
        total = total + lax.dot_general(
            wt, gain, (((0,), (0,)), ((), ())), preferred_element_type=F32
        )
    new_ref[...] = total
    both = summary_rows(
        total[:, :count],
        sorted_ref[batches + batch : batches + batch + 1, :],
        sorted_ref[2 * batches + batch : 2 * batches + batch + 1, :],
    )
    pay_ref[...] = jnp.transpose(both).astype(BF16)


def bulk_body(
    batch, first_chunk, n_in, n_out, table_ref, aw0, aw1, aw2, aw3, aw4, pcol_ref, prow_ref, *rest
):
    first = n_in == 3
    last = n_out == 2
    ins, outs, scratch = rest[:n_in], rest[n_in : n_in + n_out], rest[n_in + n_out :]
    poly_ref, band_ref, place_ref, gain_ref, part_ref, total_scratch = scratch
    aws = (aw0, aw1, aw2, aw3, aw4)
    count = pcol_ref.shape[0] // len(OFFSETS)
    members = aw0.shape[1] // 2
    padded = count + PAD
    half = table_ref[0]
    chunks = outs[0].shape[1] // CHUNK
    all_chunks = table_ref[1]
    width = all_chunks * CHUNK
    base = half * width
    middle = (base + width // 2).astype(F32) * (1.0 / RADIUS)
    position_row = prow_ref[batch : batch + 1, :]

    def entry(c, kind, what):
        return table_ref[8 + ((batch * len(KINDS) + kind) * all_chunks + c) * 2 + what]

    def centre_of(c):
        return (base + c * CHUNK + CHUNK // 2).astype(F32) * (1.0 / RADIUS)

    def weights_of(o):
        return jnp.transpose(aws[o][:count, :].astype(F32))[members:, :]

    def terms(away, reach, far):
        flat = jnp.where(far, 1.0, 0.0)
        reach = jnp.where(far, reach, 0.0)
        slope = jnp.where(away > 0.0, -2.0, 2.0) * reach
        return reach * reach, slope, flat

    wide = None
    for o in (1, 3):
        weights = weights_of(o)
        away = middle - position_row[:, o * count : (o + 1) * count]
        scaled = jnp.concatenate(
            [
                (weights * k).astype(BF16)
                for k in terms(away, 1.0 - jnp.abs(away), jnp.abs(away) < 0.5 * FAR_AWAY)
            ],
            axis=0,
        )
        part = jnp.dot(scaled, aws[o][:count, :members], preferred_element_type=F32)
        wide = part if wide is None else wide + part
    wide = [wide[r * members : (r + 1) * members, :] for r in range(3)]

    order = lax.broadcasted_iota(jnp.int32, (1, count), 1)
    for n in range(chunks):
        shift = centre_of(first_chunk + n) - middle
        part_ref[n * 3 * members : (n + 1) * 3 * members, :] = jnp.concatenate(
            [
                wide[0] + shift * (wide[1] + shift * wide[2]),
                wide[1] + (2.0 * shift) * wide[2],
                wide[2],
            ],
            axis=0,
        )
    for i, o in enumerate(KINDS):
        band_ref[i * padded : i * padded + count, :] = aws[o][:count, :]
        band_ref[i * padded + count : (i + 1) * padded, :] = jnp.zeros((PAD, 2 * members), BF16)
        at = pcol_ref[o * count : (o + 1) * count, batch : batch + 1]
        at = at + (1.0, 0.0, -1.0)[i]
        place_ref[i * padded : i * padded + count, :] = at
        place_ref[i * padded + count : (i + 1) * padded, :] = jnp.zeros((PAD, 1), F32)
        weights = weights_of(o)
        row = position_row[:, o * count : (o + 1) * count]
        scaled = []
        for n in range(chunks):
            c = first_chunk + n
            away = centre_of(c) - row
            reach = 1.0 - jnp.abs(away)
            low = entry(c, i, 0)
            high = low + WINDOW + MORE * entry(c, i, 1)
            far = (reach > 0.0) & ((order < low) | (order >= high))
            scaled += [(weights * k).astype(BF16) for k in terms(away, reach, far)]
        part = jnp.dot(
            jnp.concatenate(scaled, axis=0), aws[o][:count, :members], preferred_element_type=F32
        )
        if i + 1 < len(KINDS):
            part_ref[...] = part_ref[...] + part
        else:
            poly_ref[...] = (part_ref[...] + part).astype(BF16)

    ramp = (
        lax.broadcasted_iota(jnp.int32, (1, CHUNK), 1).astype(F32) - (CHUNK // 2)
    ) * (1.0 / RADIUS)

    def taper(kind, position, column):
        if kind == 0:
            near = jnp.maximum(position - column, 0.0)
        elif kind == 1:
            near = 1.0 - jnp.abs(column - position)
        else:
            near = jnp.maximum(column - position, 0.0)
        return near * near

    total_ref = total_scratch if last else outs[0]

    def one(n, slot):
        c = first_chunk + n
        local = pl.ds(pl.multiple_of(n * CHUNK, CHUNK), CHUNK)
        span = pl.ds(pl.multiple_of(c * CHUNK, CHUNK), CHUNK)
        if first:
            x = jnp.concatenate(
                [ins[0][:, span], ins[1][:, span].astype(F32) + ins[2][:, span]], axis=0
            )
        else:
            x = ins[0][:, span]
        mean = jnp.sum(x, axis=0, keepdims=True) * (1.0 / members)
        anom = (x - mean).astype(BF16)
        column = centre_of(c) + ramp
        starts = [pl.multiple_of(entry(c, i, 0), 16) for i in range(len(KINDS))]
        near = [band_ref[pl.ds(i * padded + starts[i], WINDOW), :] for i in range(len(KINDS))]
        poly = poly_ref[pl.ds(pl.multiple_of(n * 3 * members, 3 * members), 3 * members), :]
        lhs = jnp.concatenate([poly] + [q[:, :members] for q in near], axis=0)
        both = jnp.dot(lhs, anom, preferred_element_type=F32)
        for i in range(len(KINDS)):
            position = place_ref[pl.ds(i * padded + starts[i], WINDOW), :]
            cov = both[3 * members + i * WINDOW : 3 * members + (i + 1) * WINDOW]
            row = (slot * len(KINDS) + i) * WINDOW
            gain_ref[row : row + WINDOW, :] = (taper(i, position, column) * cov).astype(BF16)
        wt = jnp.concatenate([q[:, members:] for q in near], axis=0)
        row = slot * len(KINDS) * WINDOW
        change = lax.dot_general(
            wt,
            gain_ref[row : row + len(KINDS) * WINDOW, :],
            (((0,), (0,)), ((), ())),
            preferred_element_type=F32,
        )
        change = change + both[:members]
        change = change + ramp * (
            both[members : 2 * members] + ramp * both[2 * members : 3 * members]
        )
        return x + change, anom, column, starts, c, local

    def extend(anom, column, starts, c, local):
        for i in range(len(KINDS)):

            def more(k, carry, i=i):
                start = pl.multiple_of(i * padded + starts[i] + WINDOW + k * MORE, 16)
                aw = band_ref[pl.ds(start, MORE), :]
                cov = jnp.dot(aw[:, :members], anom, preferred_element_type=F32)
                gain = (taper(i, place_ref[pl.ds(start, MORE), :], column) * cov).astype(BF16)
                total_ref[:, local] = total_ref[:, local] + lax.dot_general(
                    aw[:, members:], gain, (((0,), (0,)), ((), ())), preferred_element_type=F32
                )
                return carry

            lax.fori_loop(0, entry(c, i, 1), more, 0)

    def pair(m, carry):
        found = [one(m * UNROLL + slot, slot) for slot in range(UNROLL)]
        for total, anom, column, starts, c, local in found:
            total_ref[:, local] = total
        for total, anom, column, starts, c, local in found:
            extend(anom, column, starts, c, local)
            if last:
                outs[0][:, local] = total_ref[: members // 2, local]
                outs[1][:, local] = total_ref[members // 2 :, local].astype(BF16)
        return carry

    lax.fori_loop(0, chunks // UNROLL, pair, 0)


def cyclic(block, distance):
    n = lax.axis_size("space")
    return lax.ppermute(block, "space", [((i + distance) % n, i) for i in range(n)])


def band(block):
    pieces = []
    for o in OFFSETS:
        pieces.append(block if o == 0 else cyclic(block, o))
    return pieces


def traded(block):
    return lax.ppermute(block, "mem", [(0, 1), (1, 0)])


def shards(state, obs_index, obs_value, obs_var):
    mem_index = lax.axis_index("mem")
    space_index = lax.axis_index("space")
    blocks = lax.axis_size("space")
    members_here, block_width = state.shape
    members = 2 * members_here
    width = block_width // 2
    batches, count = obs_index.shape

    local = obs_index - space_index * block_width
    key = local * count + lax.broadcasted_iota(jnp.int32, local.shape, 1)
    table = jnp.concatenate([key.astype(F32), local.astype(F32), obs_value, obs_var], axis=0)
    half = mem_index.astype(jnp.int32).reshape(1)
    groups = LANES // members_here
    place = local // (groups * LANES) * LANES + local % LANES
    index = jnp.concatenate([jnp.broadcast_to(half, (8,)), place.reshape(-1)])
    shape = jax.ShapeDtypeStruct
    turned, own0, srt = vmem_call(
        prep_body,
        (
            shape((block_width // groups, LANES), F32),
            shape((members_here, count), F32),
            shape((3 * batches, count), F32),
        ),
        [SM, VM, VM],
        scratch=[pltpu.VMEM((count, LANES), F32)],
        cost=cost(1e7, 6e6),
    )(index, table, state)
    other0 = traded(own0)
    own, keep, send, mean = vmem_call(
        prep_rest_body,
        (
            shape((members_here, (batches - 1) * count), F32),
            shape((members_here, width), F32),
            shape((members_here, width), BF16),
            shape((1, width), F32),
        ),
        [SM, VM, VM, VM],
        scratch=[pltpu.VMEM((count, LANES), F32)],
        cost=cost(1e7, 6e6),
    )(index, table, state, turned)
    other = traded(own)
    dev = traded(send)
    dev_mean = traded(mean)

    pay = vmem_call(
        first_body, shape((count + 16, 2 * members), BF16), [VM, VM, VM], cost=cost(1e6, 1e6)
    )(own0, other0, srt)

    aws = band(pay)
    position = jnp.stack([a[count:].astype(jnp.int32) for a in aws])
    position = position[:, :8] * LANES + position[:, 8:]
    position = position.reshape(5, count // LANES, batches, LANES).transpose(0, 2, 1, 3)
    position = position.reshape(5, batches, count)
    offset = jnp.asarray(OFFSETS, jnp.int32)
    source = space_index + offset
    valid = (source >= 0) & (source < blocks)
    relative = (position + (offset * block_width)[:, None, None]).astype(F32) * (1.0 / RADIUS)
    beyond = jnp.where(offset < 0, -FAR_AWAY, FAR_AWAY)
    relative = jnp.where(valid[:, None, None], relative, beyond[:, None, None])
    prow = relative.transpose(1, 0, 2).reshape(batches, 5 * count)
    pcol = prow.T

    chunks = width // CHUNK
    edges = mem_index * width + CHUNK * lax.iota(jnp.int32, chunks + 1)
    mixed = position[jnp.asarray(KINDS)].transpose(1, 0, 2)
    below = jnp.sum((mixed[:, :, None, :] < edges[None, None, :, None]).astype(jnp.int32), axis=-1)
    k0, k1 = below[:, :, :-1], below[:, :, 1:]
    w0 = k0 // 16 * 16
    more = jnp.maximum((k1 - w0 - WINDOW + MORE - 1) // MORE, 0)
    head = jnp.where(lax.iota(jnp.int32, 8) == 1, chunks, half)
    windows = jnp.concatenate([head, jnp.stack([w0, more], axis=-1).reshape(-1)])

    def bulk(batch, state_args, outs, first_chunk):
        kinds = len(KINDS)
        here = outs[0].shape[1] // CHUNK
        return vmem_call(
            functools.partial(bulk_body, batch, first_chunk, len(state_args), len(outs)),
            outs,
            [SM] + [VM] * (7 + len(state_args)),
            scratch=[
                pltpu.VMEM((here * 3 * members, members), BF16),
                pltpu.VMEM((kinds * (count + PAD), 2 * members), BF16),
                pltpu.VMEM((kinds * (count + PAD), 1), F32),
                pltpu.VMEM((UNROLL * kinds * WINDOW, CHUNK), BF16),
                pltpu.VMEM((here * 3 * members, members), F32),
                pltpu.VMEM((members, outs[0].shape[1] if len(outs) == 2 else LANES), F32),
            ],
            cost=cost(2e9, 6e6),
        )(windows, *aws, pcol, prow, *state_args)

    x = None
    tracked = (own, other)
    for batch in range(batches - 1):
        later = (batches - batch - 1) * count
        extra = tracked
        new, pay = vmem_call(
            functools.partial(step_body, batch + 1),
            (shape((members, later), F32), shape((count, 2 * members), BF16)),
            [VM] * (7 + len(extra)),
            cost=cost(2 * 2 * 5 * count * members * later, 1e6),
        )(*aws, pcol, srt, *extra)
        tracked = (new,)
        following = band(pay)
        state_args = (keep, dev, dev_mean) if batch == 0 else (x,)
        (x,) = bulk(batch, state_args, (shape((members, width), F32),), 0)
        aws = following

    pieces = PIECES
    mine, theirs = [], []
    for piece in range(pieces):
        size = width // pieces
        kept, sent = bulk(
            batches - 1,
            (x,),
            (shape((members_here, size), F32), shape((members_here, size), BF16)),
            piece * size // CHUNK,
        )
        mine.append(kept)
        theirs.append(traded(sent))
    mine = jnp.concatenate(mine, axis=1)
    theirs = jnp.concatenate(theirs, axis=1).astype(F32)
    first = mem_index == 0
    left = jnp.where(first, mine, theirs)
    right = jnp.where(first, theirs, mine)
    return jnp.concatenate([left, right], axis=1)


def solution(mesh):
    placed = (P("mem", "space"), P(None, "space"), P(None, "space"), P(None, "space"))
    return jax.shard_map(
        shards, mesh=mesh, in_specs=placed, out_specs=P("mem", "space"), check_vma=False
    )
```

```python
import functools

import jax
import jax.numpy as jnp
from jax import lax
from jax.experimental import pallas as pl
from jax.experimental.pallas import tpu as pltpu
from jax.sharding import PartitionSpec as P


RADIUS = 32768
OFFSETS = (-2, -1, 0, 1, 2)
CHUNK = 1024
WINDOW = 32
MORE = 128
PAD = 128
UNROLL = 2
PIECES = 2
KINDS = (0, 2, 4)
LANES = 128
FAR_AWAY = 100.0
BF16 = jnp.bfloat16
F32 = jnp.float32


def vmem_call(body, outs, ins, scratch=(), aliases=None, cost=None, room=12):
    return pl.pallas_call(
        body,
        out_shape=outs,
        in_specs=ins,
        out_specs=jax.tree.map(lambda _: pl.BlockSpec(memory_space=pltpu.VMEM), outs),
        scratch_shapes=list(scratch),
        input_output_aliases=aliases or {},
        compiler_params=pltpu.CompilerParams(vmem_limit_bytes=room << 20),
        cost_estimate=cost,
    )


VM = pl.BlockSpec(memory_space=pltpu.VMEM)
SM = pl.BlockSpec(memory_space=pltpu.SMEM)
HBM = pl.BlockSpec(memory_space=pltpu.MemorySpace.HBM)


def in_hbm(array):
    return pltpu.with_memory_space_constraint(array, pltpu.MemorySpace.HBM)


def cost(flops, moved):
    return pl.CostEstimate(flops=int(flops), bytes_accessed=int(moved), transcendentals=0)


def thirds(x):
    high = x.astype(BF16)
    rest = x - high.astype(F32)
    middle = rest.astype(BF16)
    return high, middle, (rest - middle.astype(F32)).astype(BF16)


def placement(rows, cols, b):
    count = rows.shape[1]
    rank = jnp.sum(
        jnp.where(cols[:, b : b + 1] < rows[b : b + 1], 1.0, 0.0), axis=0, keepdims=True
    )
    place = lax.broadcasted_iota(jnp.int32, (count, count), 0).astype(F32)
    return jnp.where(rank == place, 1.0, 0.0).astype(BF16)


def table_of(local, values, variances):
    key = local * local.shape[1] + lax.broadcasted_iota(jnp.int32, local.shape, 1)
    return jnp.concatenate([key.astype(F32), local.astype(F32), values, variances], axis=0)


def gather_batch(b, members, rows, cols, hot, spot_ref, turned_ref, rows_ref):
    count = rows.shape[1]
    batches = rows.shape[0] // 4
    groups = LANES // members
    unroll = 16

    def pick(i, carry):
        for u in range(unroll):
            k = i * unroll + u
            rows_ref[pl.ds(k, 1), :] = turned_ref[pl.ds(spot_ref[b, k], 1), :]
        return carry

    lax.fori_loop(0, count // unroll, pick, 0)
    group = (cols[:, batches + b : batches + b + 1].astype(jnp.int32) // LANES) % groups
    lane = lax.broadcasted_iota(jnp.int32, (count, LANES), 1) // members
    found = jnp.where(lane == group, rows_ref[...], 0.0)
    parts = [jnp.dot(hot, t, preferred_element_type=F32) for t in thirds(found)]
    placed = jnp.transpose((parts[0] + parts[1]) + parts[2])
    total = placed[:members]
    for g in range(1, groups):
        total = total + placed[g * members : (g + 1) * members]
    return total


def prep_body(
    half_ref, base_ref, index_any, value_any, var_any, x_ref,
    turned_ref, own_ref, sorted_ref, keep_ref, send0_ref, send1_ref, mean_ref, table_ref, row_ref,
    rows_ref, state_ref, index_ref, value_ref, var_ref, spot_ref, sems,
):
    half, base = half_ref[0], base_ref[0]
    members, block_width = x_ref.shape
    batches = index_ref.shape[0]
    groups = LANES // members
    width = block_width // 2
    piece = width // 2

    small = [
        pltpu.make_async_copy(source, target, sems.at[5 + i])
        for i, (source, target) in enumerate(
            ((index_any, index_ref), (value_any, value_ref), (var_any, var_ref))
        )
    ]
    for copy in small:
        copy.start()
    copies = []
    for i in range(4):
        at = pl.multiple_of(((2 - 2 * half + i) % 4) * piece, piece)
        copies.append(
            pltpu.make_async_copy(
                x_ref.at[:, pl.ds(at, piece)], state_ref.at[:, pl.ds(at, piece)], sems.at[i]
            )
        )
        copies[-1].start()
    mine = pltpu.make_async_copy(
        x_ref.at[:, pl.ds(pl.multiple_of(half * width, width), width)], keep_ref, sems.at[4]
    )
    mine.start()
    for copy in small:
        copy.wait()
    local = index_ref[...] - base
    span = groups * LANES
    row_ref[...] = local // span * LANES + local % LANES
    spots = pltpu.make_async_copy(row_ref, spot_ref, sems.at[8])
    spots.start()

    rows = table_of(local, value_ref[...], var_ref[...])
    table_ref[...] = rows
    cols = jnp.transpose(rows)
    hots = [placement(rows, cols, b) for b in range(batches)]
    for b, hot in enumerate(hots):
        values = jnp.concatenate(
            [rows[(q + 1) * batches + b : (q + 1) * batches + b + 1] for q in range(3)], axis=0
        )
        parts = [
            lax.dot_general(t, hot, (((1,), (1,)), ((), ())), preferred_element_type=F32)
            for t in thirds(values)
        ]
        ordered = (parts[0] + parts[1]) + parts[2]
        for q in range(3):
            sorted_ref[q * batches + b : q * batches + b + 1, :] = ordered[q : q + 1]

    for i in range(4):
        copies[i].wait()
        start = ((2 - 2 * half + i) % 4) * piece

        def turn(j, carry, start=start, i=i):
            at = pl.multiple_of(start + j * span, span)
            block = state_ref[:, pl.ds(at, span)]
            stack = jnp.concatenate(
                [block[:, g * LANES : (g + 1) * LANES] for g in range(groups)], axis=0
            )
            place = pl.multiple_of(start // groups + j * LANES, LANES)
            turned_ref[pl.ds(place, LANES), :] = jnp.transpose(stack)
            if i < 2:
                to = pl.ds(pl.multiple_of(i * piece + j * span, span), span)
                mean = jnp.sum(block, axis=0, keepdims=True) * (1.0 / members)
                mean_ref[:, to] = mean
                here = pl.ds(pl.multiple_of(j * span, span), span)
                (send0_ref, send1_ref)[i][:, here] = (block - mean).astype(BF16)
            return carry

        lax.fori_loop(0, piece // span, turn, 0, unroll=2)
    spots.wait()
    own_ref[...] = gather_batch(
        0, members, rows, cols, hots[0], spot_ref, turned_ref, rows_ref
    )
    mine.wait()


def prep_rest_body(spot_ref, table_ref, turned_ref, mean_ref, own_ref, rows_ref):
    batches, count = table_ref.shape[0] // 4, table_ref.shape[1]
    members = own_ref.shape[0] - mean_ref.shape[1] // own_ref.shape[1]
    rows = table_ref[...]
    cols = jnp.transpose(rows)
    for b in range(1, batches):
        hot = placement(rows, cols, b)
        own_ref[:members, (b - 1) * count : b * count] = gather_batch(
            b, members, rows, cols, hot, spot_ref, turned_ref, rows_ref
        )
    wide = own_ref.shape[1]
    own_ref[:members, (batches - 1) * count :] = jnp.zeros(
        (members, wide - (batches - 1) * count), F32
    )
    for c in range(mean_ref.shape[1] // wide):
        own_ref[members + c : members + c + 1, :] = mean_ref[:, c * wide : (c + 1) * wide]


def summary_rows(prior, values, variances):
    members = prior.shape[0]
    obs_mean = jnp.sum(prior, axis=0, keepdims=True) / members
    anomaly = prior - obs_mean
    spread = jnp.sum(anomaly * anomaly, axis=0, keepdims=True) / (members - 1) + 1e-06
    post_var = 1.0 / (1.0 / spread + 1.0 / variances)
    post_mean = post_var * (obs_mean / spread + values / variances)
    change = post_mean - obs_mean + (jnp.sqrt(post_var / spread) - 1.0) * anomaly
    weighted = change / ((members - 1) * spread)
    return jnp.concatenate([anomaly, weighted], axis=0)


def first_body(own_ref, other_ref, sorted_ref, pay_ref):
    count = sorted_ref.shape[1]
    batches = sorted_ref.shape[0] // 3
    prior = jnp.concatenate([own_ref[...], other_ref[...]], axis=0)
    both = summary_rows(
        prior, sorted_ref[batches : batches + 1, :], sorted_ref[2 * batches : 2 * batches + 1, :]
    )
    pay_ref[:count, :] = jnp.transpose(both).astype(BF16)
    pos = sorted_ref[:batches, :].astype(jnp.int32)
    pieces = [pos[:, i * LANES : (i + 1) * LANES] for i in range(count // LANES)]
    pos = jnp.concatenate(pieces, axis=0)
    pay_ref[count:, :] = jnp.concatenate(
        [(pos // LANES).astype(F32), (pos % LANES).astype(F32)], axis=0
    ).astype(BF16)


def taper_of(position, column):
    near = jnp.maximum(1.0 - jnp.abs(column - position), 0.0)
    return near * near


def step_body(batch, aw0, aw1, aw2, aw3, aw4, pcol_ref, sorted_ref, *rest):
    count = sorted_ref.shape[1]
    batches = sorted_ref.shape[0] // 3
    new_ref, pay_ref = rest[-2:]
    if batch == 1:
        have = (aw0.shape[1] // 4, (batches - 1) * count)
        old = jnp.concatenate([r[: have[0], : have[1]] for r in rest[:2]], axis=0)
    else:
        old = rest[0][:, count:]
    members = old.shape[0]
    mean = jnp.sum(old, axis=0, keepdims=True) * (1.0 / members)
    anom = (old - mean).astype(BF16)
    column = jnp.concatenate([sorted_ref[b : b + 1, :] for b in range(batch, batches)], axis=1)
    column = column * (1.0 / RADIUS)
    total = old
    for o, aw_ref in enumerate((aw0, aw1, aw2, aw3, aw4)):
        at = aw_ref[:count, :members]
        wt = aw_ref[:count, members:]
        cov = jnp.dot(at, anom, preferred_element_type=F32)
        position = pcol_ref[o * count : (o + 1) * count, batch - 1 : batch]
        gain = (taper_of(position, column) * cov).astype(BF16)
        total = total + lax.dot_general(
            wt, gain, (((0,), (0,)), ((), ())), preferred_element_type=F32
        )
    new_ref[...] = total
    both = summary_rows(
        total[:, :count],
        sorted_ref[batches + batch : batches + batch + 1, :],
        sorted_ref[2 * batches + batch : 2 * batches + batch + 1, :],
    )
    pay_ref[...] = jnp.transpose(both).astype(BF16)


def bulk_body(
    batch, all_chunks, first_chunk, skip, n_in, n_out, table_ref, aw0, aw1, aw2, aw3, aw4, pcol_ref, prow_ref, *rest
):
    first = n_in == 3
    last = n_out == 2
    ins, outs, scratch = rest[:n_in], rest[n_in : n_in + n_out], rest[n_in + n_out :]
    poly_ref, band_ref, place_ref, gain_ref, part_ref, anom_ref, total_scratch, spot_ref, dev_ref, sems = scratch
    fetch = pltpu.make_async_copy(table_ref, spot_ref, sems.at[0])
    fetch.start()
    if first:
        bring = pltpu.make_async_copy(ins[1], dev_ref, sems.at[1])
        bring.start()
    aws = (aw0, aw1, aw2, aw3, aw4)
    count = pcol_ref.shape[0] // len(OFFSETS)
    members = aw0.shape[1] // 2
    padded = count + PAD
    chunks = outs[0].shape[1] // CHUNK
    middle = all_chunks * CHUNK // 2 / RADIUS
    position_row = prow_ref[batch : batch + 1, :]

    def entry(c, kind, what):
        return spot_ref[batch, (kind * all_chunks + c) * 2 + what]

    def centre_of(c):
        if isinstance(c, int):
            return (c * CHUNK + CHUNK // 2) / RADIUS
        return (c * CHUNK + CHUNK // 2).astype(F32) * (1.0 / RADIUS)

    def weights_of(o):
        return jnp.transpose(aws[o][:count, :].astype(F32))[members:, :]

    def terms(away, reach, far):
        flat = jnp.where(far, 1.0, 0.0)
        reach = jnp.where(far, reach, 0.0)
        slope = jnp.where(away > 0.0, -2.0, 2.0) * reach
        return reach * reach, slope, flat

    wide = None
    for o in (1, 3):
        weights = weights_of(o)
        away = middle - position_row[:, o * count : (o + 1) * count]
        scaled = jnp.concatenate(
            [
                (weights * k).astype(BF16)
                for k in terms(away, 1.0 - jnp.abs(away), jnp.abs(away) < 0.5 * FAR_AWAY)
            ],
            axis=0,
        )
        part = jnp.dot(scaled, aws[o][:count, :members], preferred_element_type=F32)
        wide = part if wide is None else wide + part
    wide = [wide[r * members : (r + 1) * members, :] for r in range(3)]

    fetch.wait()

    order = lax.broadcasted_iota(jnp.int32, (1, count), 1)
    for n in range(chunks):
        shift = centre_of(first_chunk + n) - middle
        part_ref[n * 3 * members : (n + 1) * 3 * members, :] = jnp.concatenate(
            [
                wide[0] + shift * (wide[1] + shift * wide[2]),
                wide[1] + (2.0 * shift) * wide[2],
                wide[2],
            ],
            axis=0,
        )
    for i, o in enumerate(KINDS):
        band_ref[i * padded : i * padded + count, :] = aws[o][:count, :]
        band_ref[i * padded + count : (i + 1) * padded, :] = jnp.zeros((PAD, 2 * members), BF16)
        at = pcol_ref[o * count : (o + 1) * count, batch : batch + 1]
        at = at + (1.0, 0.0, -1.0)[i]
        place_ref[i * padded : i * padded + count, :] = at
        place_ref[i * padded + count : (i + 1) * padded, :] = jnp.zeros((PAD, 1), F32)
        weights = weights_of(o)
        row = position_row[:, o * count : (o + 1) * count]
        scaled = []
        for n in range(chunks):
            c = first_chunk + n
            away = centre_of(c) - row
            reach = 1.0 - jnp.abs(away)
            low = entry(c, i, 0)
            high = low + WINDOW + MORE * entry(c, i, 1)
            far = (reach > 0.0) & ((order < low) | (order >= high))
            scaled += [(weights * k).astype(BF16) for k in terms(away, reach, far)]
        part = jnp.dot(
            jnp.concatenate(scaled, axis=0), aws[o][:count, :members], preferred_element_type=F32
        )
        if i + 1 < len(KINDS):
            part_ref[...] = part_ref[...] + part
        else:
            poly_ref[...] = (part_ref[...] + part).astype(BF16)

    ramp = (
        lax.broadcasted_iota(jnp.int32, (1, CHUNK), 1).astype(F32) - (CHUNK // 2)
    ) * (1.0 / RADIUS)

    def taper(kind, position, column):
        if kind == 0:
            near = jnp.maximum(position - column, 0.0)
        elif kind == 1:
            near = 1.0 - jnp.abs(column - position)
        else:
            near = jnp.maximum(column - position, 0.0)
        return near * near

    total_ref = total_scratch if last else outs[0]

    def one(n, slot):
        c = first_chunk + n
        local = pl.ds(pl.multiple_of(n * CHUNK, CHUNK), CHUNK)
        if first:
            span = pl.ds(pl.multiple_of(c * CHUNK, CHUNK), CHUNK)
            x = jnp.concatenate(
                [
                    ins[0][:, span],
                    dev_ref[:, local].astype(F32) + ins[2][pl.ds(members // 2 + c, 1), :],
                ],
                axis=0,
            )
        else:
            x = ins[0][:, pl.ds(pl.multiple_of((skip + n) * CHUNK, CHUNK), CHUNK)]
        mean = jnp.sum(x, axis=0, keepdims=True) * (1.0 / members)
        anom = (x - mean).astype(BF16)
        anom_ref[:, local] = anom
        column = centre_of(c) + ramp
        starts = [pl.multiple_of(entry(c, i, 0), 16) for i in range(len(KINDS))]
        near = [band_ref[pl.ds(i * padded + starts[i], WINDOW), :] for i in range(len(KINDS))]
        poly = poly_ref[pl.ds(pl.multiple_of(n * 3 * members, 3 * members), 3 * members), :]
        lhs = jnp.concatenate([poly] + [q[:, :members] for q in near], axis=0)
        both = jnp.dot(lhs, anom, preferred_element_type=F32)
        for i in range(len(KINDS)):
            position = place_ref[pl.ds(i * padded + starts[i], WINDOW), :]
            cov = both[3 * members + i * WINDOW : 3 * members + (i + 1) * WINDOW]
            row = (slot * len(KINDS) + i) * WINDOW
            gain_ref[row : row + WINDOW, :] = (taper(i, position, column) * cov).astype(BF16)
        wt = jnp.concatenate([q[:, members:] for q in near], axis=0)
        row = slot * len(KINDS) * WINDOW
        change = lax.dot_general(
            wt,
            gain_ref[row : row + len(KINDS) * WINDOW, :],
            (((0,), (0,)), ((), ())),
            preferred_element_type=F32,
        )
        change = change + both[:members]
        change = change + ramp * (
            both[members : 2 * members] + ramp * both[2 * members : 3 * members]
        )
        total_ref[:, local] = x + change

    def several(m, carry):
        for slot in range(UNROLL):
            one(m * UNROLL + slot, slot)
        return carry

    if first:
        bring.wait()
    lax.fori_loop(0, chunks // UNROLL, several, 0)

    def extend(n, carry):
        c = first_chunk + n
        local = pl.ds(pl.multiple_of(n * CHUNK, CHUNK), CHUNK)
        column = centre_of(c) + ramp
        for i in range(len(KINDS)):

            def more(k, carry, i=i):
                start = pl.multiple_of(i * padded + entry(c, i, 0) + WINDOW + k * MORE, 16)
                aw = band_ref[pl.ds(start, MORE), :]
                cov = jnp.dot(aw[:, :members], anom_ref[:, local], preferred_element_type=F32)
                gain = (taper(i, place_ref[pl.ds(start, MORE), :], column) * cov).astype(BF16)
                total_ref[:, local] = total_ref[:, local] + lax.dot_general(
                    aw[:, members:], gain, (((0,), (0,)), ((), ())), preferred_element_type=F32
                )
                return carry

            lax.fori_loop(0, entry(c, i, 1), more, 0)
        if last:
            outs[0][:, local] = total_ref[: members // 2, local]
            outs[1][:, local] = total_ref[members // 2 :, local].astype(BF16)
        return carry

    lax.fori_loop(0, chunks, extend, 0)


def cyclic(block, distance):
    n = lax.axis_size("space")
    return lax.ppermute(block, "space", [((i + distance) % n, i) for i in range(n)])


def band(block):
    pieces = []
    for o in OFFSETS:
        pieces.append(block if o == 0 else cyclic(block, o))
    return pieces


def traded(block):
    return lax.ppermute(block, "mem", [(0, 1), (1, 0)])


def shards(state, obs_index, obs_value, obs_var):
    mem_index = lax.axis_index("mem")
    space_index = lax.axis_index("space")
    blocks = lax.axis_size("space")
    members_here, block_width = state.shape
    members = 2 * members_here
    width = block_width // 2
    batches, count = obs_index.shape

    half = mem_index.astype(jnp.int32).reshape(1)
    base = (space_index * block_width).astype(jnp.int32).reshape(1)
    groups = LANES // members_here
    part = width // PIECES
    shape = jax.ShapeDtypeStruct
    turned, own0, srt, keep, send0, send1, mean, sort_table, spots = vmem_call(
        prep_body,
        (
            shape((block_width // groups, LANES), F32),
            shape((members_here, count), F32),
            shape((3 * batches, count), F32),
            shape((members_here, width), F32),
            shape((members_here, part), BF16),
            shape((members_here, part), BF16),
            shape((1, width), F32),
            shape((4 * batches, count), F32),
            shape((batches, count), jnp.int32),
        ),
        [SM, SM, HBM, HBM, HBM, HBM],
        scratch=[
            pltpu.VMEM((count, LANES), F32),
            pltpu.VMEM((members_here, block_width), F32),
            pltpu.VMEM((batches, count), jnp.int32),
            pltpu.VMEM((batches, count), F32),
            pltpu.VMEM((batches, count), F32),
            pltpu.SMEM((batches, count), jnp.int32),
            pltpu.SemaphoreType.DMA((9,)),
        ],
        cost=cost(1e7, 6e6),
    )(half, base, *(in_hbm(a) for a in (obs_index, obs_value, obs_var, state)))
    other0 = traded(own0)
    devs = [traded(send) for send in (send0, send1)]
    own = vmem_call(
        prep_rest_body,
        shape((members_here + width // CHUNK, CHUNK), F32),
        [SM, VM, VM, VM],
        scratch=[pltpu.VMEM((count, LANES), F32)],
        cost=cost(1e7, 6e6),
    )(spots, sort_table, turned, mean)
    other = traded(own)

    pay = vmem_call(
        first_body, shape((count + 16, 2 * members), BF16), [VM, VM, VM], cost=cost(1e6, 1e6)
    )(own0, other0, srt)

    aws = band(pay)
    position = jnp.stack([a[count:].astype(jnp.int32) for a in aws])
    position = position[:, :8] * LANES + position[:, 8:]
    position = position.reshape(5, count // LANES, batches, LANES).transpose(0, 2, 1, 3)
    position = position.reshape(5, batches, count)
    offset = jnp.asarray(OFFSETS, jnp.int32)
    source = space_index + offset
    valid = (source >= 0) & (source < blocks)
    relative = (position + (offset * block_width)[:, None, None]).astype(F32) * (1.0 / RADIUS)
    beyond = jnp.where(offset < 0, -FAR_AWAY, FAR_AWAY)
    relative = jnp.where(valid[:, None, None], relative, beyond[:, None, None])
    prow = relative.transpose(1, 0, 2).reshape(batches, 5 * count)
    pcol = prow.T

    chunks = width // CHUNK
    edges = mem_index * width + CHUNK * lax.iota(jnp.int32, chunks + 1)
    mixed = position[jnp.asarray(KINDS)].transpose(1, 0, 2)
    below = jnp.sum((mixed[:, :, None, :] < edges[None, None, :, None]).astype(jnp.int32), axis=-1)
    k0, k1 = below[:, :, :-1], below[:, :, 1:]
    w0 = k0 // 16 * 16
    more = jnp.maximum((k1 - w0 - WINDOW + MORE - 1) // MORE, 0)
    table = jnp.stack([w0, more], axis=-1).reshape(batches, -1)
    table = jnp.pad(table, ((0, 8 - batches), (0, LANES - table.shape[1])))
    start = (mem_index * width).astype(F32) * (1.0 / RADIUS)
    brow, bcol = prow - start, pcol - start

    def bulk(batch, aws, state_args, outs, first_chunk):
        kinds = len(KINDS)
        here = outs[0].shape[1] // CHUNK
        return vmem_call(
            functools.partial(bulk_body, batch, width // CHUNK, *first_chunk, len(state_args), len(outs)),
            outs,
            [VM] * 8 + ([VM, HBM, VM] if len(state_args) == 3 else [VM]),
            scratch=[
                pltpu.VMEM((here * 3 * members, members), BF16),
                pltpu.VMEM((kinds * (count + PAD), 2 * members), BF16),
                pltpu.VMEM((kinds * (count + PAD), 1), F32),
                pltpu.VMEM((UNROLL * kinds * WINDOW, CHUNK), BF16),
                pltpu.VMEM((here * 3 * members, members), F32),
                pltpu.VMEM((members, outs[0].shape[1]), BF16),
                pltpu.VMEM((members, outs[0].shape[1] if len(outs) == 2 else LANES), F32),
                pltpu.SMEM((8, LANES), jnp.int32),
                pltpu.VMEM((members_here, part) if len(state_args) == 3 else (16, LANES), BF16),
                pltpu.SemaphoreType.DMA((2,)),
            ],
            cost=cost(2e9, 6e6),
        )(table, *aws, bcol, brow, *state_args)

    every = []
    tracked = (own, other)
    for batch in range(batches - 1):
        later = (batches - batch - 1) * count
        extra = tracked
        new, pay = vmem_call(
            functools.partial(step_body, batch + 1),
            (shape((members, later), F32), shape((count, 2 * members), BF16)),
            [VM] * (7 + len(extra)),
            cost=cost(2 * 2 * 5 * count * members * later, 1e6),
        )(*aws, pcol, srt, *extra)
        tracked = (new,)
        following = band(pay)
        every.append(aws)
        aws = following
    every.append(aws)

    mine, theirs = [], []
    for piece in range(PIECES):
        x = (keep, devs[piece], other)
        for batch in range(batches - 1):
            x = bulk(
                batch, every[batch], x, (shape((members, part), F32),), (piece * part // CHUNK, 0)
            )
        parts = 2 if piece == PIECES - 1 else 1
        size = part // parts
        for p in range(parts):
            kept, sent = bulk(
                batches - 1,
                every[-1],
                x,
                (shape((members_here, size), F32), shape((members_here, size), BF16)),
                ((piece * part + p * size) // CHUNK, p * size // CHUNK),
            )
            mine.append(kept)
            theirs.append(traded(sent))
    mine = jnp.concatenate(mine, axis=1)
    theirs = jnp.concatenate(theirs, axis=1).astype(F32)
    first = mem_index == 0
    left = jnp.where(first, mine, theirs)
    right = jnp.where(first, theirs, mine)
    return jnp.concatenate([left, right], axis=1)


def solution(mesh):
    placed = (P("mem", "space"), P(None, "space"), P(None, "space"), P(None, "space"))
    return jax.shard_map(
        shards, mesh=mesh, in_specs=placed, out_specs=P("mem", "space"), check_vma=False
    )
```

```python
import functools

import jax
import jax.numpy as jnp
from jax import lax
from jax.experimental import pallas as pl
from jax.experimental.pallas import tpu as pltpu
from jax.sharding import PartitionSpec as P


RADIUS = 32768
OFFSETS = (-2, -1, 0, 1, 2)
CHUNK = 1024
WINDOW = 32
MORE = 128
PAD = 128
UNROLL = 4
PIECES = 2
KINDS = (0, 2, 4)
LANES = 128
FAR_AWAY = 100.0
BF16 = jnp.bfloat16
F32 = jnp.float32


def vmem_call(body, outs, ins, scratch=(), aliases=None, cost=None, room=12):
    return pl.pallas_call(
        body,
        out_shape=outs,
        in_specs=ins,
        out_specs=jax.tree.map(lambda _: pl.BlockSpec(memory_space=pltpu.VMEM), outs),
        scratch_shapes=list(scratch),
        input_output_aliases=aliases or {},
        compiler_params=pltpu.CompilerParams(vmem_limit_bytes=room << 20),
        cost_estimate=cost,
    )


VM = pl.BlockSpec(memory_space=pltpu.VMEM)
SM = pl.BlockSpec(memory_space=pltpu.SMEM)
HBM = pl.BlockSpec(memory_space=pltpu.MemorySpace.HBM)


def in_hbm(array):
    return pltpu.with_memory_space_constraint(array, pltpu.MemorySpace.HBM)


def cost(flops, moved):
    return pl.CostEstimate(flops=int(flops), bytes_accessed=int(moved), transcendentals=0)


def thirds(x):
    high = x.astype(BF16)
    rest = x - high.astype(F32)
    middle = rest.astype(BF16)
    return high, middle, (rest - middle.astype(F32)).astype(BF16)


def placement(rows, cols, b):
    count = rows.shape[1]
    rank = jnp.sum(
        jnp.where(cols[:, b : b + 1] < rows[b : b + 1], 1.0, 0.0), axis=0, keepdims=True
    )
    place = lax.broadcasted_iota(jnp.int32, (count, count), 0).astype(F32)
    return jnp.where(rank == place, 1.0, 0.0).astype(BF16)


def table_of(local, values, variances):
    key = local * local.shape[1] + lax.broadcasted_iota(jnp.int32, local.shape, 1)
    return jnp.concatenate([key.astype(F32), local.astype(F32), values, variances], axis=0)


def gather_batch(b, members, rows, cols, hot, spot_ref, turned_ref, rows_ref):
    count = rows.shape[1]
    batches = rows.shape[0] // 4
    groups = LANES // members
    unroll = 16

    def pick(i, carry):
        for u in range(unroll):
            k = i * unroll + u
            rows_ref[pl.ds(k, 1), :] = turned_ref[pl.ds(spot_ref[b, k], 1), :]
        return carry

    lax.fori_loop(0, count // unroll, pick, 0)
    group = (cols[:, batches + b : batches + b + 1].astype(jnp.int32) // LANES) % groups
    lane = lax.broadcasted_iota(jnp.int32, (count, LANES), 1) // members
    found = jnp.where(lane == group, rows_ref[...], 0.0)
    parts = [jnp.dot(hot, t, preferred_element_type=F32) for t in thirds(found)]
    placed = jnp.transpose((parts[0] + parts[1]) + parts[2])
    total = placed[:members]
    for g in range(1, groups):
        total = total + placed[g * members : (g + 1) * members]
    return total


def prep_body(
    half_ref, base_ref, index_any, value_any, var_any, x_ref,
    turned_ref, own_ref, sorted_ref, keep_ref, send0_ref, send1_ref, mean_ref, table_ref, row_ref,
    rows_ref, state_ref, index_ref, value_ref, var_ref, spot_ref, sems,
):
    half, base = half_ref[0], base_ref[0]
    members, block_width = x_ref.shape
    batches = index_ref.shape[0]
    groups = LANES // members
    width = block_width // 2
    piece = width // 2

    small = [
        pltpu.make_async_copy(source, target, sems.at[5 + i])
        for i, (source, target) in enumerate(
            ((index_any, index_ref), (value_any, value_ref), (var_any, var_ref))
        )
    ]
    for copy in small:
        copy.start()
    copies = []
    for i in range(4):
        at = pl.multiple_of(((2 - 2 * half + i) % 4) * piece, piece)
        copies.append(
            pltpu.make_async_copy(
                x_ref.at[:, pl.ds(at, piece)], state_ref.at[:, pl.ds(at, piece)], sems.at[i]
            )
        )
        copies[-1].start()
    mine = pltpu.make_async_copy(
        x_ref.at[:, pl.ds(pl.multiple_of(half * width, width), width)], keep_ref, sems.at[4]
    )
    mine.start()
    for copy in small:
        copy.wait()
    local = index_ref[...] - base
    span = groups * LANES
    row_ref[...] = local // span * LANES + local % LANES
    spots = pltpu.make_async_copy(row_ref, spot_ref, sems.at[8])
    spots.start()

    rows = table_of(local, value_ref[...], var_ref[...])
    table_ref[...] = rows
    cols = jnp.transpose(rows)
    hots = [placement(rows, cols, b) for b in range(batches)]
    for b, hot in enumerate(hots):
        values = jnp.concatenate(
            [rows[(q + 1) * batches + b : (q + 1) * batches + b + 1] for q in range(3)], axis=0
        )
        parts = [
            lax.dot_general(t, hot, (((1,), (1,)), ((), ())), preferred_element_type=F32)
            for t in thirds(values)
        ]
        ordered = (parts[0] + parts[1]) + parts[2]
        for q in range(3):
            sorted_ref[q * batches + b : q * batches + b + 1, :] = ordered[q : q + 1]

    for i in range(4):
        copies[i].wait()
        start = ((2 - 2 * half + i) % 4) * piece

        def turn(j, carry, start=start, i=i):
            at = pl.multiple_of(start + j * span, span)
            block = state_ref[:, pl.ds(at, span)]
            stack = jnp.concatenate(
                [block[:, g * LANES : (g + 1) * LANES] for g in range(groups)], axis=0
            )
            place = pl.multiple_of(start // groups + j * LANES, LANES)
            turned_ref[pl.ds(place, LANES), :] = jnp.transpose(stack)
            if i < 2:
                to = pl.ds(pl.multiple_of(i * piece + j * span, span), span)
                mean = jnp.sum(block, axis=0, keepdims=True) * (1.0 / members)
                mean_ref[:, to] = mean
                here = pl.ds(pl.multiple_of(j * span, span), span)
                (send0_ref, send1_ref)[i][:, here] = (block - mean).astype(BF16)
            return carry

        lax.fori_loop(0, piece // span, turn, 0, unroll=2)
    spots.wait()
    own_ref[...] = gather_batch(
        0, members, rows, cols, hots[0], spot_ref, turned_ref, rows_ref
    )
    mine.wait()


def prep_rest_body(spot_ref, table_ref, turned_ref, mean_ref, own_ref, rows_ref):
    batches, count = table_ref.shape[0] // 4, table_ref.shape[1]
    members = own_ref.shape[0] - mean_ref.shape[1] // own_ref.shape[1]
    rows = table_ref[...]
    cols = jnp.transpose(rows)
    for b in range(1, batches):
        hot = placement(rows, cols, b)
        own_ref[:members, (b - 1) * count : b * count] = gather_batch(
            b, members, rows, cols, hot, spot_ref, turned_ref, rows_ref
        )
    wide = own_ref.shape[1]
    own_ref[:members, (batches - 1) * count :] = jnp.zeros(
        (members, wide - (batches - 1) * count), F32
    )
    for c in range(mean_ref.shape[1] // wide):
        own_ref[members + c : members + c + 1, :] = mean_ref[:, c * wide : (c + 1) * wide]


def summary_rows(prior, values, variances):
    members = prior.shape[0]
    obs_mean = jnp.sum(prior, axis=0, keepdims=True) / members
    anomaly = prior - obs_mean
    spread = jnp.sum(anomaly * anomaly, axis=0, keepdims=True) / (members - 1) + 1e-06
    post_var = 1.0 / (1.0 / spread + 1.0 / variances)
    post_mean = post_var * (obs_mean / spread + values / variances)
    change = post_mean - obs_mean + (jnp.sqrt(post_var / spread) - 1.0) * anomaly
    weighted = change / ((members - 1) * spread)
    return jnp.concatenate([anomaly, weighted], axis=0)


def first_body(own_ref, other_ref, sorted_ref, pay_ref):
    count = sorted_ref.shape[1]
    batches = sorted_ref.shape[0] // 3
    prior = jnp.concatenate([own_ref[...], other_ref[...]], axis=0)
    both = summary_rows(
        prior, sorted_ref[batches : batches + 1, :], sorted_ref[2 * batches : 2 * batches + 1, :]
    )
    pay_ref[:count, :] = jnp.transpose(both).astype(BF16)
    pos = sorted_ref[:batches, :].astype(jnp.int32)
    pieces = [pos[:, i * LANES : (i + 1) * LANES] for i in range(count // LANES)]
    pos = jnp.concatenate(pieces, axis=0)
    pay_ref[count:, :] = jnp.concatenate(
        [(pos // LANES).astype(F32), (pos % LANES).astype(F32)], axis=0
    ).astype(BF16)


def taper_of(position, column):
    near = jnp.maximum(1.0 - jnp.abs(column - position), 0.0)
    return near * near


def step_body(batch, aw0, aw1, aw2, aw3, aw4, pcol_ref, sorted_ref, *rest):
    count = sorted_ref.shape[1]
    batches = sorted_ref.shape[0] // 3
    new_ref, pay_ref = rest[-2:]
    if batch == 1:
        have = (aw0.shape[1] // 4, (batches - 1) * count)
        old = jnp.concatenate([r[: have[0], : have[1]] for r in rest[:2]], axis=0)
    else:
        old = rest[0][:, count:]
    members = old.shape[0]
    mean = jnp.sum(old, axis=0, keepdims=True) * (1.0 / members)
    anom = (old - mean).astype(BF16)
    column = jnp.concatenate([sorted_ref[b : b + 1, :] for b in range(batch, batches)], axis=1)
    column = column * (1.0 / RADIUS)
    total = old
    for o, aw_ref in enumerate((aw0, aw1, aw2, aw3, aw4)):
        at = aw_ref[:count, :members]
        wt = aw_ref[:count, members:]
        cov = jnp.dot(at, anom, preferred_element_type=F32)
        position = pcol_ref[o * count : (o + 1) * count, batch - 1 : batch]
        gain = (taper_of(position, column) * cov).astype(BF16)
        total = total + lax.dot_general(
            wt, gain, (((0,), (0,)), ((), ())), preferred_element_type=F32
        )
    new_ref[...] = total
    both = summary_rows(
        total[:, :count],
        sorted_ref[batches + batch : batches + batch + 1, :],
        sorted_ref[2 * batches + batch : 2 * batches + batch + 1, :],
    )
    pay_ref[...] = jnp.transpose(both).astype(BF16)


def bulk_body(
    batch, all_chunks, first_chunk, skip, n_in, n_out, table_ref, aw0, aw1, aw2, aw3, aw4, pcol_ref, prow_ref, *rest
):
    first = n_in == 3
    last = n_out == 2
    ins, outs, scratch = rest[:n_in], rest[n_in : n_in + n_out], rest[n_in + n_out :]
    poly_ref, band_ref, place_ref, gain_ref, part_ref, anom_ref, total_scratch, spot_ref, dev_ref, sems = scratch
    fetch = pltpu.make_async_copy(table_ref, spot_ref, sems.at[0])
    fetch.start()
    if first:
        bring = pltpu.make_async_copy(ins[1], dev_ref, sems.at[1])
        bring.start()
    aws = (aw0, aw1, aw2, aw3, aw4)
    count = pcol_ref.shape[0] // len(OFFSETS)
    members = aw0.shape[1] // 2
    padded = count + PAD
    chunks = outs[0].shape[1] // CHUNK
    middle = all_chunks * CHUNK // 2 / RADIUS
    unroll = min(UNROLL, chunks)
    position_row = prow_ref[batch : batch + 1, :]

    def entry(c, kind, what):
        return spot_ref[batch, (kind * all_chunks + c) * 2 + what]

    def centre_of(c):
        if isinstance(c, int):
            return (c * CHUNK + CHUNK // 2) / RADIUS
        return (c * CHUNK + CHUNK // 2).astype(F32) * (1.0 / RADIUS)

    def weights_of(o):
        return jnp.transpose(aws[o][:count, :].astype(F32))[members:, :]

    def terms(away, reach, far):
        flat = jnp.where(far, 1.0, 0.0)
        reach = jnp.where(far, reach, 0.0)
        slope = jnp.where(away > 0.0, -2.0, 2.0) * reach
        return reach * reach, slope, flat

    wide = None
    for o in (1, 3):
        weights = weights_of(o)
        away = middle - position_row[:, o * count : (o + 1) * count]
        scaled = jnp.concatenate(
            [
                (weights * k).astype(BF16)
                for k in terms(away, 1.0 - jnp.abs(away), jnp.abs(away) < 0.5 * FAR_AWAY)
            ],
            axis=0,
        )
        part = jnp.dot(scaled, aws[o][:count, :members], preferred_element_type=F32)
        wide = part if wide is None else wide + part
    wide = [wide[r * members : (r + 1) * members, :] for r in range(3)]

    fetch.wait()

    order = lax.broadcasted_iota(jnp.int32, (1, count), 1)
    for n in range(chunks):
        shift = centre_of(first_chunk + n) - middle
        part_ref[n * 3 * members : (n + 1) * 3 * members, :] = jnp.concatenate(
            [
                wide[0] + shift * (wide[1] + shift * wide[2]),
                wide[1] + (2.0 * shift) * wide[2],
                wide[2],
            ],
            axis=0,
        )
    for i, o in enumerate(KINDS):
        band_ref[i * padded : i * padded + count, :] = aws[o][:count, :]
        band_ref[i * padded + count : (i + 1) * padded, :] = jnp.zeros((PAD, 2 * members), BF16)
        at = pcol_ref[o * count : (o + 1) * count, batch : batch + 1]
        at = at + (1.0, 0.0, -1.0)[i]
        place_ref[i * padded : i * padded + count, :] = at
        place_ref[i * padded + count : (i + 1) * padded, :] = jnp.zeros((PAD, 1), F32)
        weights = weights_of(o)
        row = position_row[:, o * count : (o + 1) * count]
        scaled = []
        for n in range(chunks):
            c = first_chunk + n
            away = centre_of(c) - row
            reach = 1.0 - jnp.abs(away)
            low = entry(c, i, 0)
            high = low + WINDOW + MORE * entry(c, i, 1)
            far = (reach > 0.0) & ((order < low) | (order >= high))
            scaled += [(weights * k).astype(BF16) for k in terms(away, reach, far)]
        part = jnp.dot(
            jnp.concatenate(scaled, axis=0), aws[o][:count, :members], preferred_element_type=F32
        )
        if i + 1 < len(KINDS):
            part_ref[...] = part_ref[...] + part
        else:
            poly_ref[...] = (part_ref[...] + part).astype(BF16)

    ramp = (
        lax.broadcasted_iota(jnp.int32, (1, CHUNK), 1).astype(F32) - (CHUNK // 2)
    ) * (1.0 / RADIUS)

    def taper(kind, position, column):
        if kind == 0:
            near = jnp.maximum(position - column, 0.0)
        elif kind == 1:
            near = 1.0 - jnp.abs(column - position)
        else:
            near = jnp.maximum(column - position, 0.0)
        return near * near

    total_ref = total_scratch if last else outs[0]

    def one(n, slot):
        c = first_chunk + n
        local = pl.ds(pl.multiple_of(n * CHUNK, CHUNK), CHUNK)
        if first:
            span = pl.ds(pl.multiple_of(c * CHUNK, CHUNK), CHUNK)
            x = jnp.concatenate(
                [
                    ins[0][:, span],
                    dev_ref[:, local].astype(F32) + ins[2][pl.ds(members // 2 + c, 1), :],
                ],
                axis=0,
            )
        else:
            x = ins[0][:, pl.ds(pl.multiple_of((skip + n) * CHUNK, CHUNK), CHUNK)]
        mean = jnp.sum(x, axis=0, keepdims=True) * (1.0 / members)
        anom = (x - mean).astype(BF16)
        anom_ref[:, local] = anom
        column = centre_of(c) + ramp
        starts = [pl.multiple_of(entry(c, i, 0), 16) for i in range(len(KINDS))]
        near = [band_ref[pl.ds(i * padded + starts[i], WINDOW), :] for i in range(len(KINDS))]
        poly = poly_ref[pl.ds(pl.multiple_of(n * 3 * members, 3 * members), 3 * members), :]
        lhs = jnp.concatenate([poly] + [q[:, :members] for q in near], axis=0)
        both = jnp.dot(lhs, anom, preferred_element_type=F32)
        for i in range(len(KINDS)):
            position = place_ref[pl.ds(i * padded + starts[i], WINDOW), :]
            cov = both[3 * members + i * WINDOW : 3 * members + (i + 1) * WINDOW]
            row = (slot * len(KINDS) + i) * WINDOW
            gain_ref[row : row + WINDOW, :] = (taper(i, position, column) * cov).astype(BF16)
        wt = jnp.concatenate([q[:, members:] for q in near], axis=0)
        row = slot * len(KINDS) * WINDOW
        change = lax.dot_general(
            wt,
            gain_ref[row : row + len(KINDS) * WINDOW, :],
            (((0,), (0,)), ((), ())),
            preferred_element_type=F32,
        )
        change = change + both[:members]
        change = change + ramp * (
            both[members : 2 * members] + ramp * both[2 * members : 3 * members]
        )
        total_ref[:, local] = x + change

    def several(m, carry):
        for slot in range(unroll):
            one(m * unroll + slot, slot)
        return carry

    if first:
        bring.wait()
    lax.fori_loop(0, chunks // unroll, several, 0)

    def extend(n, carry):
        c = first_chunk + n
        local = pl.ds(pl.multiple_of(n * CHUNK, CHUNK), CHUNK)
        column = centre_of(c) + ramp
        for i in range(len(KINDS)):

            def more(k, carry, i=i):
                start = pl.multiple_of(i * padded + entry(c, i, 0) + WINDOW + k * MORE, 16)
                aw = band_ref[pl.ds(start, MORE), :]
                cov = jnp.dot(aw[:, :members], anom_ref[:, local], preferred_element_type=F32)
                gain = (taper(i, place_ref[pl.ds(start, MORE), :], column) * cov).astype(BF16)
                total_ref[:, local] = total_ref[:, local] + lax.dot_general(
                    aw[:, members:], gain, (((0,), (0,)), ((), ())), preferred_element_type=F32
                )
                return carry

            lax.fori_loop(0, entry(c, i, 1), more, 0)
        if last:
            outs[0][:, local] = total_ref[: members // 2, local]
            outs[1][:, local] = total_ref[members // 2 :, local].astype(BF16)
        return carry

    lax.fori_loop(0, chunks, extend, 0)


def cyclic(block, distance):
    n = lax.axis_size("space")
    return lax.ppermute(block, "space", [((i + distance) % n, i) for i in range(n)])


def band(block):
    pieces = []
    for o in OFFSETS:
        pieces.append(block if o == 0 else cyclic(block, o))
    return pieces


def traded(block):
    return lax.ppermute(block, "mem", [(0, 1), (1, 0)])


def shards(state, obs_index, obs_value, obs_var):
    mem_index = lax.axis_index("mem")
    space_index = lax.axis_index("space")
    blocks = lax.axis_size("space")
    members_here, block_width = state.shape
    members = 2 * members_here
    width = block_width // 2
    batches, count = obs_index.shape

    half = mem_index.astype(jnp.int32).reshape(1)
    base = (space_index * block_width).astype(jnp.int32).reshape(1)
    groups = LANES // members_here
    part = width // PIECES
    shape = jax.ShapeDtypeStruct
    turned, own0, srt, keep, send0, send1, mean, sort_table, spots = vmem_call(
        prep_body,
        (
            shape((block_width // groups, LANES), F32),
            shape((members_here, count), F32),
            shape((3 * batches, count), F32),
            shape((members_here, width), F32),
            shape((members_here, part), BF16),
            shape((members_here, part), BF16),
            shape((1, width), F32),
            shape((4 * batches, count), F32),
            shape((batches, count), jnp.int32),
        ),
        [SM, SM, HBM, HBM, HBM, HBM],
        scratch=[
            pltpu.VMEM((count, LANES), F32),
            pltpu.VMEM((members_here, block_width), F32),
            pltpu.VMEM((batches, count), jnp.int32),
            pltpu.VMEM((batches, count), F32),
            pltpu.VMEM((batches, count), F32),
            pltpu.SMEM((batches, count), jnp.int32),
            pltpu.SemaphoreType.DMA((9,)),
        ],
        cost=cost(1e7, 6e6),
    )(half, base, *(in_hbm(a) for a in (obs_index, obs_value, obs_var, state)))
    other0 = traded(own0)
    devs = [traded(send) for send in (send0, send1)]
    own = vmem_call(
        prep_rest_body,
        shape((members_here + width // CHUNK, CHUNK), F32),
        [SM, VM, VM, VM],
        scratch=[pltpu.VMEM((count, LANES), F32)],
        cost=cost(1e7, 6e6),
    )(spots, sort_table, turned, mean)
    other = traded(own)

    pay = vmem_call(
        first_body, shape((count + 16, 2 * members), BF16), [VM, VM, VM], cost=cost(1e6, 1e6)
    )(own0, other0, srt)

    aws = band(pay)
    position = jnp.stack([a[count:].astype(jnp.int32) for a in aws])
    position = position[:, :8] * LANES + position[:, 8:]
    position = position.reshape(5, count // LANES, batches, LANES).transpose(0, 2, 1, 3)
    position = position.reshape(5, batches, count)
    offset = jnp.asarray(OFFSETS, jnp.int32)
    source = space_index + offset
    valid = (source >= 0) & (source < blocks)
    relative = (position + (offset * block_width)[:, None, None]).astype(F32) * (1.0 / RADIUS)
    beyond = jnp.where(offset < 0, -FAR_AWAY, FAR_AWAY)
    relative = jnp.where(valid[:, None, None], relative, beyond[:, None, None])
    prow = relative.transpose(1, 0, 2).reshape(batches, 5 * count)
    pcol = prow.T

    chunks = width // CHUNK
    edges = mem_index * width + CHUNK * lax.iota(jnp.int32, chunks + 1)
    mixed = position[jnp.asarray(KINDS)].transpose(1, 0, 2)
    below = jnp.sum((mixed[:, :, None, :] < edges[None, None, :, None]).astype(jnp.int32), axis=-1)
    k0, k1 = below[:, :, :-1], below[:, :, 1:]
    w0 = k0 // 16 * 16
    more = jnp.maximum((k1 - w0 - WINDOW + MORE - 1) // MORE, 0)
    table = jnp.stack([w0, more], axis=-1).reshape(batches, -1)
    table = jnp.pad(table, ((0, 8 - batches), (0, LANES - table.shape[1])))
    start = (mem_index * width).astype(F32) * (1.0 / RADIUS)
    brow, bcol = prow - start, pcol - start

    def bulk(batch, aws, state_args, outs, first_chunk):
        kinds = len(KINDS)
        here = outs[0].shape[1] // CHUNK
        return vmem_call(
            functools.partial(bulk_body, batch, width // CHUNK, *first_chunk, len(state_args), len(outs)),
            outs,
            [VM] * 8 + ([VM, HBM, VM] if len(state_args) == 3 else [VM]),
            scratch=[
                pltpu.VMEM((here * 3 * members, members), BF16),
                pltpu.VMEM((kinds * (count + PAD), 2 * members), BF16),
                pltpu.VMEM((kinds * (count + PAD), 1), F32),
                pltpu.VMEM((UNROLL * kinds * WINDOW, CHUNK), BF16),
                pltpu.VMEM((here * 3 * members, members), F32),
                pltpu.VMEM((members, outs[0].shape[1]), BF16),
                pltpu.VMEM((members, outs[0].shape[1] if len(outs) == 2 else LANES), F32),
                pltpu.SMEM((8, LANES), jnp.int32),
                pltpu.VMEM((members_here, part) if len(state_args) == 3 else (16, LANES), BF16),
                pltpu.SemaphoreType.DMA((2,)),
            ],
            cost=cost(2e9, 6e6),
        )(table, *aws, bcol, brow, *state_args)

    every = []
    tracked = (own, other)
    for batch in range(batches - 1):
        later = (batches - batch - 1) * count
        extra = tracked
        new, pay = vmem_call(
            functools.partial(step_body, batch + 1),
            (shape((members, later), F32), shape((count, 2 * members), BF16)),
            [VM] * (7 + len(extra)),
            cost=cost(2 * 2 * 5 * count * members * later, 1e6),
        )(*aws, pcol, srt, *extra)
        tracked = (new,)
        following = band(pay)
        every.append(aws)
        aws = following
    every.append(aws)

    mine, theirs = [], []
    for piece in range(PIECES):
        x = (keep, devs[piece], other)
        for batch in range(batches - 1):
            x = bulk(
                batch, every[batch], x, (shape((members, part), F32),), (piece * part // CHUNK, 0)
            )
        parts = 2 if piece == PIECES - 1 else 1
        size = part // parts
        for p in range(parts):
            kept, sent = bulk(
                batches - 1,
                every[-1],
                x,
                (shape((members_here, size), F32), shape((members_here, size), BF16)),
                ((piece * part + p * size) // CHUNK, p * size // CHUNK),
            )
            mine.append(kept)
            theirs.append(traded(sent))
    mine = jnp.concatenate(mine, axis=1)
    theirs = jnp.concatenate(theirs, axis=1).astype(F32)
    first = mem_index == 0
    left = jnp.where(first, mine, theirs)
    right = jnp.where(first, theirs, mine)
    return jnp.concatenate([left, right], axis=1)


def solution(mesh):
    placed = (P("mem", "space"), P(None, "space"), P(None, "space"), P(None, "space"))
    return jax.shard_map(
        shards, mesh=mesh, in_specs=placed, out_specs=P("mem", "space"), check_vma=False
    )
```
